32 devices in a mesh: groups: 2 (over x), expert: 16 (over z, y, core).
Axes of the slice: x: 2, y: 2, z: 4, core: 2. Of those that a mesh axis runs over, the one named last changes fastest.
Arguments:
- residual: bfloat16 [512, 2880], P(('groups', 'expert')), parts along dimension 0, may hold values from -6 to 6
- norm_gain: float32 [2880], replicated, may hold values from 0.1 to 1.9
- expert_ids: int32 [512, 4], P(('groups', 'expert')), parts along dimension 0, may hold values from 0 to 7, all different within a row; in each aligned block of 16 rows (0 to 15, 16 to 31, ...) at most 16 rows name the same one
- expert_weights: float32 [512, 4], P(('groups', 'expert')), parts along dimension 0, may hold values from 0.2 to 1
- gate_proj: bfloat16 [16, 2880, 720], P('expert'), may hold values from -0.109375 to 0.109375
- up_proj: bfloat16 [16, 2880, 720], P('expert'), may hold values from -0.109375 to 0.109375
- down_proj: bfloat16 [16, 720, 2880], P('expert'), may hold values from -0.15625 to 0.15625
Outputs:
- mixed: bfloat16 [512, 2880], P(('groups', 'expert')), parts along dimension 0
The draws below stay inside these ranges and needn't reach their ends.
There are 2 independent parts, one for each index of `groups`. The reference program is written for one: setup_inputs(seed, part) draws one part's arguments, and reference() takes and returns one part's arrays. A program takes and returns all parts, laid end to end along the dimension named above; an argument that names none is the same for every part. Nothing has to cross between parts.
Inputs may be any that keep to these rules, and one draw needn't show every extreme that they name: `expert_ids`: in each aligned block of 16 rows (the rows of one device) no expert is named by more than 16 entries.
All inputs are finite; a program needn't handle non-finite values.
Results may differ from the reference program's by a relative error of at most 0.0063.
Values may be sent and summed in bfloat16 or wider, within the bound.
A program may use at most 64 MiB of HBM per device.

```python
import math
import jax
import jax.numpy as jnp
import numpy as np
from jax import lax

D = 2880
FF = 1440
HALF = 720
TOP = 4
EXPERTS = 8
REQ_DEV = 16
CAP = 16
TOKENS = 256
N_EXPERT = 16


def block_levels(key, dims, pieces, low, largest):
    def one(position, blocks):
        steps = jax.random.uniform(jax.random.fold_in(jax.random.fold_in(key, 6), position), (blocks,), jnp.float32, low / len(pieces), largest / len(pieces))
        return jnp.repeat(jnp.exp(steps), dims[position] // blocks).reshape((-1,) + (1,) * (len(dims) - position - 1))

    factor_of = one(*pieces[0])
    for cut in pieces[1:]:
        factor_of = factor_of * one(*cut)
    return factor_of


def deal_out(own_key, own, number, rows, count, top, bound, lean):
    sequence = jax.random.permutation(own_key, count)
    packed, usual = portions_of(count, rows * top, bound, lean, True), portions_of(count, rows * top, bound, lean, False)
    places = jnp.arange(count)

    def named(sizes, rotation):
        used = int((sizes > 0).sum())
        fixed = max(1, used // 4)
        shifted = fixed + (places - fixed + rotation * (used - fixed)) % max(1, count - fixed)
        return jnp.zeros((count,), jnp.int32).at[sequence[jnp.where(places < fixed, places, shifted)]].set(jnp.asarray(sizes, jnp.int32))

    sizes = jnp.where(number % 4 == 0, named(packed, number // 4), named(usual, number - number // 4 - 1))
    mixed = jax.random.permutation(jax.random.fold_in(own, 3), count)
    donor, taker = mixed[0:count // 2 * 2:2], mixed[1:count // 2 * 2:2]
    room = jnp.minimum(sizes[donor] - 1, bound - sizes[taker]) // 2
    room = jnp.where((donor == sequence[0]) | (taker == sequence[0]) | (sizes[taker] == 0), 0, jnp.maximum(room, 0))
    shifted = jax.random.randint(jax.random.fold_in(own, 4), (count // 2,), 0, 1 << 20) % (room + 1)
    sizes = sizes.at[donor].add(-shifted).at[taker].add(shifted)
    items = jnp.searchsorted(jnp.cumsum(sizes), jnp.arange(rows * top), side="right").astype(jnp.int32)
    grid = items.reshape(top, rows).T
    grid = grid[jax.random.permutation(jax.random.fold_in(own, 1), rows)]
    rotation = jax.random.randint(jax.random.fold_in(own, 2), (rows, 1), 0, top)
    return jnp.take_along_axis(grid, (jnp.arange(top)[None, :] + rotation) % top, axis=1)


def portions_of(amount, total, most, lean, full):
    loads = [(1 << 20) // math.isqrt(grade ** lean) + 1 for grade in range(1, amount + 1)]
    largest = most if full else min(most, max(-(-total // amount), total * loads[0] // sum(loads)))
    least = 1 if total - largest >= amount - 1 else 0
    counts, rest = [largest] + [least] * (amount - 1), total - largest - least * (amount - 1)
    while rest > 0:
        candidates = [i for i in range(1, amount) if counts[i] < largest] or [i for i in range(1, amount) if counts[i] < most]
        pool, left = sum([loads[i] for i in candidates]), rest
        for i in candidates:
            addition = min(most - counts[i], max(1, left * loads[i] // pool), rest)
            counts[i] = counts[i] + addition
            rest = rest - addition
    return np.array(counts)


def normal_values(stream_key, shape, scale, bound, shards=(), dtype=jnp.bfloat16):
    factor_of = block_levels(stream_key, shape, shards, -0.22, 0.18) if shards else 1.0
    array = jax.random.normal(stream_key, shape, jnp.float32) * scale * factor_of
    return jnp.minimum(jnp.maximum(array, -bound), bound).astype(dtype)


def setup_inputs(seed: int = 0, part: int = 0) -> dict:
    streams_of = jax.random.split(jax.random.key(seed), 8)
    own_keys = jax.random.split(jax.random.fold_in(streams_of[7], part), 8)
    residual = normal_values(own_keys[0], (TOKENS, D), 1.0, 6.0, ((0, 16),))
    norm_gain = jnp.clip(1.0 + 0.18 * jax.random.normal(streams_of[1], (D,), jnp.float32), 0.1, 1.9)
    expert_ids_keys = jax.random.split(jax.random.fold_in(own_keys[2], 1), TOKENS // REQ_DEV)
    expert_ids_turns = jax.random.permutation(jax.random.fold_in(own_keys[2], 3), TOKENS // REQ_DEV)
    expert_ids = jax.vmap(lambda own, number: deal_out(jax.random.fold_in(own_keys[2], 2), own, number, REQ_DEV, EXPERTS, TOP, CAP, 2))(expert_ids_keys, expert_ids_turns).reshape((TOKENS, TOP))
    expert_weights = jnp.clip(0.2 + 0.8 * jax.random.uniform(own_keys[3], (TOKENS, TOP), jnp.float32) ** block_levels(own_keys[3], (TOKENS, TOP), ((0, 16),), -0.2, 0.2), 0.2, 1.0)
    gate_proj = normal_values(streams_of[4], (2 * EXPERTS, D, HALF), D ** -0.5, 0.109375, ((0, 16),))
    up_proj = normal_values(streams_of[5], (2 * EXPERTS, D, HALF), D ** -0.5, 0.109375, ((0, 16),))
    down_proj = normal_values(streams_of[6], (2 * EXPERTS, HALF, D), FF ** -0.5, 0.15625, ((0, 16),))
    return {"residual": residual, "norm_gain": norm_gain, "expert_ids": expert_ids, "expert_weights": expert_weights, "gate_proj": gate_proj, "up_proj": up_proj, "down_proj": down_proj}


def expert_half(flat, gate_w, up_w, down_w):
    gate = jnp.dot(flat, gate_w, preferred_element_type=jnp.float32)
    upper = jnp.dot(flat, up_w, preferred_element_type=jnp.float32)
    act = (gate * jax.nn.sigmoid(1.702 * gate) * (upper + 1.0)).astype(jnp.bfloat16)
    return jnp.dot(act, down_w, preferred_element_type=jnp.float32).astype(jnp.bfloat16)

def reference(residual, norm_gain, expert_ids, expert_weights, gate_proj, up_proj, down_proj):
    devices = N_EXPERT
    experts = devices // 2
    width = REQ_DEV * TOP
    x = residual.astype(jnp.float32)
    scale = lax.rsqrt(lax.optimization_barrier(jnp.mean(x * x, axis=-1, keepdims=True)) + 1e-05)
    normed = (x * scale * norm_gain.astype(jnp.float32)).astype(jnp.bfloat16)
    flat = expert_ids.reshape(devices, width).astype(jnp.int32)
    onehot = (flat[:, :, None] == jnp.arange(experts).astype(jnp.int32)[None, None, :]).astype(jnp.int32)
    slot = (lax.optimization_barrier(jnp.sum(onehot * jnp.cumsum(onehot, axis=1), axis=-1)) - 1).astype(jnp.int32)
    source = jnp.broadcast_to(jnp.arange(devices).astype(jnp.int32)[:, None], (devices, width))
    token = (jnp.arange(width).astype(jnp.int32) // TOP)[None, :] + source * REQ_DEV
    buffer = jnp.zeros((experts, devices, CAP, D), jnp.bfloat16).at[flat, source, slot].set(normed[token])

    def run(items):
        block, gate_w, up_w, down_w = items
        first = expert_half(block, gate_w[0], up_w[0], down_w[0])
        second = expert_half(block, gate_w[1], up_w[1], down_w[1])
        return (first.astype(jnp.float32) + second.astype(jnp.float32)).astype(jnp.bfloat16)
    outs = lax.map(run, (buffer.reshape(experts, devices * CAP, D), gate_proj.reshape(experts, 2, D, HALF), up_proj.reshape(experts, 2, D, HALF), down_proj.reshape(experts, 2, HALF, D)))
    outs = outs.reshape(experts, devices, CAP, D)
    picked = outs[flat, source, slot].reshape(devices, REQ_DEV, TOP, D).astype(jnp.float32)
    weights = expert_weights.reshape(devices, REQ_DEV, TOP, 1)
    mixed = x.reshape(devices, REQ_DEV, D) + lax.optimization_barrier(jnp.sum(weights * picked, axis=2))
    return mixed.reshape(TOKENS, D).astype(jnp.bfloat16)
```

```python
import functools

import jax
import jax.numpy as jnp
from jax import lax
from jax.experimental import pallas as pl
from jax.experimental.pallas import tpu as pltpu
from jax.sharding import PartitionSpec as P

BF16 = jnp.bfloat16
F32 = jnp.float32
LANES = 128


def partner(value, axis, bit):
    mask = 2**bit
    pairs = [(source, source ^ mask) for source in range(lax.axis_size(axis))]
    return lax.ppermute(value, axis, pairs)


def expert_half(block, gate_w, up_w, down_w):
    flat = block.reshape(-1, block.shape[-1])
    gate = jnp.dot(flat, gate_w, preferred_element_type=jnp.float32)
    upper = jnp.dot(flat, up_w, preferred_element_type=jnp.float32)
    act = (gate * jax.nn.sigmoid(1.702 * gate) * (upper + 1.0)).astype(jnp.bfloat16)
    out = jnp.dot(act, down_w, preferred_element_type=jnp.float32).astype(jnp.bfloat16)
    return out.reshape(block.shape[:-1] + (down_w.shape[1],))


def slotted(residual, norm_gain, expert_ids, expert_weights, gate_proj, up_proj, down_proj):
    rows, model = residual.shape
    chosen = expert_ids.shape[1]
    devices = lax.axis_size("expert")
    experts = devices // 2
    capacity = 2 * rows * chosen // experts
    half_cap = capacity // 2
    gate_w, up_w, down_w = (gate_proj[0], up_proj[0], down_proj[0])
    x = residual.astype(jnp.float32)
    scale = lax.rsqrt(jnp.mean(x * x, axis=-1, keepdims=True) + 1e-05)
    normed = (x * scale * norm_gain).astype(jnp.bfloat16)
    flat_ids = expert_ids.reshape(rows * chosen)
    onehot = (
        flat_ids[:, None] == lax.broadcasted_iota(jnp.int32, (rows * chosen, experts), 1)
    ).astype(jnp.int32)
    slot = jnp.sum(onehot * jnp.cumsum(onehot, axis=0), axis=1) - 1
    position = flat_ids * capacity + slot
    pick = (
        position[:, None] == lax.broadcasted_iota(jnp.int32, (rows * chosen, experts * capacity), 1)
    ).astype(jnp.float32)
    place_rows = jnp.sum(pick.reshape(rows, chosen, experts * capacity), axis=1)
    send = lax.dot_general(
        place_rows.astype(jnp.bfloat16),
        normed,
        (((0,), (0,)), ((), ())),
        preferred_element_type=jnp.float32,
    )
    send = send.astype(jnp.bfloat16).reshape(experts, capacity, model)
    outgoing = send.reshape(experts, 2, half_cap, model).reshape(devices, half_cap, model)
    arrived = lax.all_to_all(outgoing, "expert", split_axis=0, concat_axis=0, tiled=True)
    other = partner(arrived, "expert", 0)
    both = expert_half(jnp.stack((arrived, other)), gate_w, up_w, down_w)
    returned = partner(both[1], "expert", 0)
    finished = (both[0].astype(jnp.float32) + returned.astype(jnp.float32)).astype(jnp.bfloat16)
    back = lax.all_to_all(finished, "expert", split_axis=0, concat_axis=0, tiled=True)
    results = back.reshape(experts, capacity, model)
    weighted = jnp.sum(
        (pick * expert_weights.reshape(rows * chosen)[:, None]).reshape(
            rows, chosen, experts * capacity
        ),
        axis=1,
    )
    combined = jnp.dot(
        weighted,
        results.reshape(experts * capacity, model).astype(jnp.float32),
        precision=lax.Precision.HIGHEST,
    )
    return (x + combined).astype(jnp.bfloat16)


def cuts(total, pieces):
    step = -(-total // (pieces * 2 * LANES)) * 2 * LANES
    return [(start, min(step, total - start)) for start in range(0, total, step)]


def kernel(
    line, experts, in_cuts, out_cuts,
    res_ref, gain_ref, ids_ref, wts_ref, gate_hbm, up_hbm, down_hbm, out_ref,
    gate_v, up_v, down_v, xg, gacc, uacc, part, core_r, y_s, y_r, z_s, z_r,
    w_sem, d_sem, agz_s, agz_r, agy_s, agy_r, agc_s, agc_r,
    rc_s, rc_r, ry_s, ry_r, rz_s, rz_r,
):
    rows, model = res_ref.shape
    extra = xg.shape[1] - model
    me = lax.axis_index("expert")
    core = lax.rem(me, 2)
    y = lax.rem(me // 2, 2)
    z = me // 4

    def device(z_, y_, c_):
        return (z_ * 2 + y_) * 2 + c_

    def row(z_, y_, c_):
        return pl.multiple_of(((c_ * 2 + y_) * line + z_) * rows, rows)

    def z_at(offset):
        return lax.rem(z + offset + line, line)

    def remote(src, dst, send, recv, target):
        return pltpu.make_async_remote_copy(
            src_ref=src, dst_ref=dst, send_sem=send, recv_sem=recv,
            device_id={"expert": target}, device_id_type=pl.DeviceIdType.MESH,
        )

    y_dev = device(z, 1 - y, core)
    c_dev = device(z, y, 1 - core)

    loads = []
    for k, (at, wide) in enumerate(in_cuts):
        pair = []
        for n, (hbm, vmem) in enumerate(((gate_hbm, gate_v), (up_hbm, up_v))):
            copy = pltpu.make_async_copy(
                hbm.at[0, pl.ds(at, wide), :], vmem.at[pl.ds(at, wide), :], w_sem.at[k, n]
            )
            copy.start()
            pair.append(copy)
        loads.append(pair)
    down_load = pltpu.make_async_copy(down_hbm.at[0], down_v, d_sem)
    down_load.start()

    barrier = pltpu.get_barrier_semaphore()
    peers = [device(z_at(o), y, core) for o in range(1, line)] + [y_dev, c_dev]
    for peer in peers:
        pl.semaphore_signal(
            barrier, inc=1, device_id={"expert": peer}, device_id_type=pl.DeviceIdType.MESH
        )

    mine = row(z, y, core)
    x = res_ref[...].astype(F32)
    scale = lax.rsqrt(jnp.mean(x * x, axis=-1, keepdims=True) + 1e-05)
    xg[pl.ds(mine, rows), 0:model] = (x * scale * gain_ref[...]).astype(BF16)
    lane = lax.broadcasted_iota(jnp.int32, (rows, extra), 1)
    high = jnp.zeros((rows, extra), F32)
    low = jnp.zeros((rows, extra), F32)
    for k in range(ids_ref.shape[1]):
        ids = ids_ref[:, k : k + 1]
        high = high + jnp.where(ids == lane, wts_ref[:, k : k + 1], 0.0)
        low = low + jnp.where(ids + experts == lane, wts_ref[:, k : k + 1], 0.0)
    rest = low - low.astype(BF16).astype(F32)
    xg[pl.ds(mine, rows), model : model + extra] = (high + rest).astype(BF16)

    pl.semaphore_wait(barrier, len(peers))

    sent = []

    def go(copy):
        copy.start()
        sent.append(copy)

    spans = []
    for k, (at, wide) in enumerate(in_cuts):
        if k == len(in_cuts) - 1:
            wide = wide + extra
        spans.append((at, wide))

    def block(z_, y_, c_, count, k):
        at, wide = spans[k]
        return xg.at[pl.ds(row(z_, y_, c_), count * rows), pl.ds(at, wide)]

    chunks = len(in_cuts)
    for k in range(chunks):
        own = block(z, y, core, 1, k)
        for o in range(1, line):
            go(remote(own, own, agz_s.at[k, o], agz_r.at[k, o], device(z_at(o), y, core)))
        go(remote(own, own, agy_s.at[k, 0], agy_r.at[k, 0], y_dev))

    def relay_z(k):
        for o in range(1, line):
            got = block(z_at(-o), y, core, 1, k)
            remote(got, got, agz_s.at[k, o], agz_r.at[k, o], me).wait_recv()
            go(remote(got, got, agy_s.at[k, o], agy_r.at[k, o], y_dev))
        group = block(0, y, core, line, k)
        go(remote(group, group, agc_s.at[k, 0], agc_r.at[k, 0], c_dev))

    def relay_y(k):
        for o in range(line):
            got = block(z_at(-o), 1 - y, core, 1, k)
            remote(got, got, agy_s.at[k, o], agy_r.at[k, o], y_dev).wait_recv()
        group = block(0, 1 - y, core, line, k)
        go(remote(group, group, agc_s.at[k, 1], agc_r.at[k, 1], c_dev))

    def arrive(k):
        for n, y_ in enumerate((y, 1 - y)):
            group = block(0, y_, 1 - core, line, k)
            remote(group, group, agc_s.at[k, n], agc_r.at[k, n], c_dev).wait_recv()

    def multiply(k):
        at, wide = in_cuts[k]
        tokens = xg[:, at : at + wide]
        for n, (vmem, acc) in enumerate(((gate_v, gacc), (up_v, uacc))):
            loads[k][n].wait()
            product = jnp.dot(tokens, vmem[at : at + wide, :], preferred_element_type=F32)
            if k == 0:
                acc[...] = product
            else:
                acc[...] += product

    relay_z(0)
    for k in range(chunks):
        relay_y(k)
        if k + 1 < chunks:
            relay_z(k + 1)
        arrive(k)
        multiply(k)

    gate = gacc[...]
    act = (gate * jax.nn.sigmoid(1.702 * gate) * (uacc[...] + 1.0)).astype(BF16)
    expert = me // 2
    lanes = lax.broadcasted_iota(jnp.int32, (xg.shape[0], extra), 1)
    ours = jnp.logical_or(lanes == expert, lanes == expert + experts)
    weight = jnp.sum(
        jnp.where(ours, xg[:, model : model + extra].astype(F32), 0.0), axis=1, keepdims=True
    )
    down_load.wait()

    half = 2 * line * rows
    quarter = line * rows
    my_half = pl.multiple_of(core * half, half)
    its_half = pl.multiple_of((1 - core) * half, half)
    my_y = pl.multiple_of(y * quarter, quarter)
    its_y = pl.multiple_of((1 - y) * quarter, quarter)
    my_z = pl.multiple_of(z * rows, rows)

    def core_copy(j):
        at, wide = out_cuts[j]
        cols = pl.ds(at, wide)
        return remote(
            part.at[pl.ds(its_half, half), cols], core_r.at[:, cols],
            rc_s.at[j], rc_r.at[j], c_dev,
        )

    def y_copy(j):
        at, wide = out_cuts[j]
        cols = pl.ds(at, wide)
        return remote(y_s.at[:, cols], y_r.at[:, cols], ry_s.at[j], ry_r.at[j], y_dev)

    def z_copy(j, o):
        at, wide = out_cuts[j]
        cols = pl.ds(at, wide)
        there = pl.multiple_of(z_at(o) * rows, rows)
        return remote(
            z_s.at[pl.ds(there, rows), cols], z_r.at[o, :, cols],
            rz_s.at[j, o], rz_r.at[j, o], device(z_at(o), y, core),
        )

    def first(j):
        at, wide = out_cuts[j]
        product = jnp.dot(act, down_v[:, at : at + wide], preferred_element_type=F32)
        part[:, at : at + wide] = (product * weight).astype(BF16)
        go(core_copy(j))

    def second(j):
        at, wide = out_cuts[j]
        core_copy(j).wait_recv()
        theirs = core_r[pl.ds(its_y, quarter), at : at + wide].astype(F32)
        here = part[pl.ds(my_half + its_y, quarter), at : at + wide].astype(F32)
        y_s[:, at : at + wide] = (theirs + here).astype(BF16)
        go(y_copy(j))

    def third(j):
        at, wide = out_cuts[j]
        theirs = core_r[pl.ds(my_y, quarter), at : at + wide].astype(F32)
        here = part[pl.ds(my_half + my_y, quarter), at : at + wide].astype(F32)
        y_copy(j).wait_recv()
        total = theirs + here + y_r[:, at : at + wide].astype(F32)
        z_s[:, at : at + wide] = total.astype(BF16)
        for o in range(1, line):
            go(z_copy(j, o))

    def fourth(j):
        at, wide = out_cuts[j]
        total = z_s[pl.ds(my_z, rows), at : at + wide].astype(F32)
        for o in range(1, line):
            z_copy(j, o).wait_recv()
            total = total + z_r[o, :, at : at + wide].astype(F32)
        out_ref[:, at : at + wide] = (
            res_ref[:, at : at + wide].astype(F32) + total
        ).astype(BF16)

    pieces = len(out_cuts)
    for step in range(pieces + 3):
        for lag, stage in enumerate((first, second, third, fourth)):
            if 0 <= step - lag < pieces:
                stage(step - lag)
    for copy in sent:
        copy.wait_send()


def fused(residual, norm_gain, expert_ids, expert_weights, gate_proj, up_proj, down_proj):
    rows, model = residual.shape
    hidden = gate_proj.shape[2]
    devices = lax.axis_size("expert")
    experts = devices // 2
    line = devices // 4
    tokens = rows * devices
    width = -(-(model + 2 * experts) // LANES) * LANES
    in_cuts = cuts(model, 3)
    out_cuts = cuts(model, 3)
    ins, outs = len(in_cuts), len(out_cuts)
    vmem = pl.BlockSpec(memory_space=pltpu.VMEM)
    hbm = pl.BlockSpec(memory_space=pl.ANY)
    dma = pltpu.SemaphoreType.DMA
    return pl.pallas_call(
        functools.partial(kernel, line, experts, in_cuts, out_cuts),
        out_shape=jax.ShapeDtypeStruct((rows, model), BF16),
        in_specs=[vmem] * 4 + [hbm] * 3,
        out_specs=vmem,
        scratch_shapes=[
            pltpu.VMEM((model, hidden), BF16),
            pltpu.VMEM((model, hidden), BF16),
            pltpu.VMEM((hidden, model), BF16),
            pltpu.VMEM((tokens, width), BF16),
            pltpu.VMEM((tokens, hidden), F32),
            pltpu.VMEM((tokens, hidden), F32),
            pltpu.VMEM((tokens, model), BF16),
            pltpu.VMEM((tokens // 2, model), BF16),
            pltpu.VMEM((tokens // 4, model), BF16),
            pltpu.VMEM((tokens // 4, model), BF16),
            pltpu.VMEM((tokens // 4, model), BF16),
            pltpu.VMEM((line, rows, model), BF16),
            dma((ins, 2)),
            dma,
            dma((ins, line)),
            dma((ins, line)),
            dma((ins, line)),
            dma((ins, line)),
            dma((ins, 2)),
            dma((ins, 2)),
            dma((outs,)),
            dma((outs,)),
            dma((outs,)),
            dma((outs,)),
            dma((outs, line)),
            dma((outs, line)),
        ],
        compiler_params=pltpu.CompilerParams(
            collective_id=0, has_side_effects=True, vmem_limit_bytes=60 * 1024 * 1024
        ),
    )(
        residual, norm_gain.reshape(1, model), expert_ids, expert_weights,
        gate_proj, up_proj, down_proj,
    )


def body(residual, norm_gain, expert_ids, expert_weights, gate_proj, up_proj, down_proj):
    rows = residual.shape[0]
    devices = lax.axis_size("expert")
    capacity = 4 * rows * expert_ids.shape[1] // devices
    dense = capacity >= rows and devices % 4 == 0
    form = fused if dense else slotted
    return form(
        residual, norm_gain, expert_ids, expert_weights, gate_proj, up_proj, down_proj
    )


def solution(mesh):
    in_specs = (
        P(("groups", "expert"), None),
        P(),
        P(("groups", "expert"), None),
        P(("groups", "expert"), None),
        P("expert", None, None),
        P("expert", None, None),
        P("expert", None, None),
    )
    out_specs = P(("groups", "expert"), None)
    return jax.shard_map(body, mesh=mesh, in_specs=in_specs, out_specs=out_specs, check_vma=False)
```

```python
import functools

import jax
import jax.numpy as jnp
from jax import lax
from jax.experimental import pallas as pl
from jax.experimental.pallas import tpu as pltpu
from jax.sharding import PartitionSpec as P

BF16 = jnp.bfloat16
F32 = jnp.float32
LANES = 128


def partner(value, axis, bit):
    mask = 2**bit
    pairs = [(source, source ^ mask) for source in range(lax.axis_size(axis))]
    return lax.ppermute(value, axis, pairs)


def expert_half(block, gate_w, up_w, down_w):
    flat = block.reshape(-1, block.shape[-1])
    gate = jnp.dot(flat, gate_w, preferred_element_type=jnp.float32)
    upper = jnp.dot(flat, up_w, preferred_element_type=jnp.float32)
    act = (gate * jax.nn.sigmoid(1.702 * gate) * (upper + 1.0)).astype(jnp.bfloat16)
    out = jnp.dot(act, down_w, preferred_element_type=jnp.float32).astype(jnp.bfloat16)
    return out.reshape(block.shape[:-1] + (down_w.shape[1],))


def slotted(residual, norm_gain, expert_ids, expert_weights, gate_proj, up_proj, down_proj):
    rows, model = residual.shape
    chosen = expert_ids.shape[1]
    devices = lax.axis_size("expert")
    experts = devices // 2
    capacity = 2 * rows * chosen // experts
    half_cap = capacity // 2
    gate_w, up_w, down_w = (gate_proj[0], up_proj[0], down_proj[0])
    x = residual.astype(jnp.float32)
    scale = lax.rsqrt(jnp.mean(x * x, axis=-1, keepdims=True) + 1e-05)
    normed = (x * scale * norm_gain).astype(jnp.bfloat16)
    flat_ids = expert_ids.reshape(rows * chosen)
    onehot = (
        flat_ids[:, None] == lax.broadcasted_iota(jnp.int32, (rows * chosen, experts), 1)
    ).astype(jnp.int32)
    slot = jnp.sum(onehot * jnp.cumsum(onehot, axis=0), axis=1) - 1
    position = flat_ids * capacity + slot
    pick = (
        position[:, None] == lax.broadcasted_iota(jnp.int32, (rows * chosen, experts * capacity), 1)
    ).astype(jnp.float32)
    place_rows = jnp.sum(pick.reshape(rows, chosen, experts * capacity), axis=1)
    send = lax.dot_general(
        place_rows.astype(jnp.bfloat16),
        normed,
        (((0,), (0,)), ((), ())),
        preferred_element_type=jnp.float32,
    )
    send = send.astype(jnp.bfloat16).reshape(experts, capacity, model)
    outgoing = send.reshape(experts, 2, half_cap, model).reshape(devices, half_cap, model)
    arrived = lax.all_to_all(outgoing, "expert", split_axis=0, concat_axis=0, tiled=True)
    other = partner(arrived, "expert", 0)
    both = expert_half(jnp.stack((arrived, other)), gate_w, up_w, down_w)
    returned = partner(both[1], "expert", 0)
    finished = (both[0].astype(jnp.float32) + returned.astype(jnp.float32)).astype(jnp.bfloat16)
    back = lax.all_to_all(finished, "expert", split_axis=0, concat_axis=0, tiled=True)
    results = back.reshape(experts, capacity, model)
    weighted = jnp.sum(
        (pick * expert_weights.reshape(rows * chosen)[:, None]).reshape(
            rows, chosen, experts * capacity
        ),
        axis=1,
    )
    combined = jnp.dot(
        weighted,
        results.reshape(experts * capacity, model).astype(jnp.float32),
        precision=lax.Precision.HIGHEST,
    )
    return (x + combined).astype(jnp.bfloat16)


def cuts(total, pieces):
    step = -(-total // (pieces * 2 * LANES)) * 2 * LANES
    return [(start, min(step, total - start)) for start in range(0, total, step)]


def kernel(
    line, experts, in_cuts, out_cuts,
    res_ref, gain_ref, ids_ref, wts_ref, gate_hbm, up_hbm, down_hbm, out_ref,
    gate_v, up_v, down_v, xg, gacc, uacc, part, core_r, y_s, y_r, z_s, z_r,
    w_sem, d_sem, agz_s, agz_r, agy_s, agy_r, agc_s, agc_r,
    rc_s, rc_r, ry_s, ry_r, rz_s, rz_r,
):
    rows, model = res_ref.shape
    extra = xg.shape[1] - model
    me = lax.axis_index("expert")
    core = lax.rem(me, 2)
    y = lax.rem(me // 2, 2)
    z = me // 4

    def device(z_, y_, c_):
        return (z_ * 2 + y_) * 2 + c_

    def row(z_, y_, c_):
        return pl.multiple_of(((c_ * 2 + y_) * line + z_) * rows, rows)

    def z_at(offset):
        return lax.rem(z + offset + line, line)

    def remote(src, dst, send, recv, target):
        return pltpu.make_async_remote_copy(
            src_ref=src, dst_ref=dst, send_sem=send, recv_sem=recv,
            device_id={"expert": target}, device_id_type=pl.DeviceIdType.MESH,
        )

    y_dev = device(z, 1 - y, core)
    c_dev = device(z, y, 1 - core)

    loads = []
    for k, (at, wide) in enumerate(in_cuts):
        pair = []
        for n, (hbm, vmem) in enumerate(((gate_hbm, gate_v), (up_hbm, up_v))):
            copy = pltpu.make_async_copy(
                hbm.at[0, :, pl.ds(at, wide)], vmem.at[:, pl.ds(at, wide)], w_sem.at[k, n]
            )
            copy.start()
            pair.append(copy)
        loads.append(pair)
    down_load = pltpu.make_async_copy(down_hbm.at[0], down_v, d_sem)
    down_load.start()

    barrier = pltpu.get_barrier_semaphore()
    peers = [device(z_at(o), y, core) for o in range(1, line)] + [y_dev, c_dev]
    for peer in peers:
        pl.semaphore_signal(
            barrier, inc=1, device_id={"expert": peer}, device_id_type=pl.DeviceIdType.MESH
        )

    mine = row(z, y, core)
    x = res_ref[...].astype(F32)
    scale = lax.rsqrt(jnp.mean(x * x, axis=-1, keepdims=True) + 1e-05)
    xg[pl.ds(mine, rows), 0:model] = (x * scale * gain_ref[...]).astype(BF16)
    named = lax.broadcasted_iota(jnp.int32, (extra, rows), 0)
    high = jnp.zeros((extra, rows), F32)
    low = jnp.zeros((extra, rows), F32)
    for k in range(ids_ref.shape[0]):
        ids = ids_ref[k : k + 1, :]
        high = high + jnp.where(ids == named, wts_ref[k : k + 1, :], 0.0)
        low = low + jnp.where(ids + experts == named, wts_ref[k : k + 1, :], 0.0)
    rest = low - low.astype(BF16).astype(F32)
    xg[pl.ds(mine, rows), model : model + extra] = jnp.transpose(high + rest).astype(BF16)

    pl.semaphore_wait(barrier, len(peers))

    sent = []

    def go(copy):
        copy.start()
        sent.append(copy)

    spans = []
    for k, (at, wide) in enumerate(in_cuts):
        if k == len(in_cuts) - 1:
            wide = wide + extra
        spans.append((at, wide))

    def block(z_, y_, c_, count, k):
        at, wide = spans[k]
        return xg.at[pl.ds(row(z_, y_, c_), count * rows), pl.ds(at, wide)]

    chunks = len(in_cuts)
    for k in range(chunks):
        own = block(z, y, core, 1, k)
        for o in range(1, line):
            go(remote(own, own, agz_s.at[k, o], agz_r.at[k, o], device(z_at(o), y, core)))
        go(remote(own, own, agy_s.at[k, 0], agy_r.at[k, 0], y_dev))

    def relay_z(k):
        for o in range(1, line):
            got = block(z_at(-o), y, core, 1, k)
            remote(got, got, agz_s.at[k, o], agz_r.at[k, o], me).wait_recv()
            go(remote(got, got, agy_s.at[k, o], agy_r.at[k, o], y_dev))
        group = block(0, y, core, line, k)
        go(remote(group, group, agc_s.at[k, 0], agc_r.at[k, 0], c_dev))

    def relay_y(k):
        for o in range(line):
            got = block(z_at(-o), 1 - y, core, 1, k)
            remote(got, got, agy_s.at[k, o], agy_r.at[k, o], y_dev).wait_recv()
        group = block(0, 1 - y, core, line, k)
        go(remote(group, group, agc_s.at[k, 1], agc_r.at[k, 1], c_dev))

    def arrive(k):
        for n, y_ in enumerate((y, 1 - y)):
            group = block(0, y_, 1 - core, line, k)
            remote(group, group, agc_s.at[k, n], agc_r.at[k, n], c_dev).wait_recv()

    def multiply(k):
        at, wide = in_cuts[k]
        tokens = xg[:, at : at + wide]
        for n, (vmem, acc) in enumerate(((gate_v, gacc), (up_v, uacc))):
            loads[k][n].wait()
            product = lax.dot_general(
                tokens, vmem[:, at : at + wide], (((1,), (1,)), ((), ())),
                preferred_element_type=F32,
            )
            if k == 0:
                acc[...] = product
            else:
                acc[...] += product

    relay_z(0)
    for k in range(chunks):
        relay_y(k)
        if k + 1 < chunks:
            relay_z(k + 1)
        arrive(k)
        multiply(k)

    gate = gacc[...]
    act = (gate * jax.nn.sigmoid(1.702 * gate) * (uacc[...] + 1.0)).astype(BF16)
    expert = me // 2
    lanes = lax.broadcasted_iota(jnp.int32, (xg.shape[0], extra), 1)
    ours = jnp.logical_or(lanes == expert, lanes == expert + experts)
    weight = jnp.sum(
        jnp.where(ours, xg[:, model : model + extra].astype(F32), 0.0), axis=1, keepdims=True
    )
    down_load.wait()

    half = 2 * line * rows
    quarter = line * rows
    my_half = pl.multiple_of(core * half, half)
    its_half = pl.multiple_of((1 - core) * half, half)
    my_y = pl.multiple_of(y * quarter, quarter)
    its_y = pl.multiple_of((1 - y) * quarter, quarter)
    my_z = pl.multiple_of(z * rows, rows)

    def core_copy(j):
        at, wide = out_cuts[j]
        cols = pl.ds(at, wide)
        return remote(
            part.at[pl.ds(its_half, half), cols], core_r.at[:, cols],
            rc_s.at[j], rc_r.at[j], c_dev,
        )

    def y_copy(j):
        at, wide = out_cuts[j]
        cols = pl.ds(at, wide)
        return remote(y_s.at[:, cols], y_r.at[:, cols], ry_s.at[j], ry_r.at[j], y_dev)

    def z_copy(j, o):
        at, wide = out_cuts[j]
        cols = pl.ds(at, wide)
        there = pl.multiple_of(z_at(o) * rows, rows)
        return remote(
            z_s.at[pl.ds(there, rows), cols], z_r.at[o, :, cols],
            rz_s.at[j, o], rz_r.at[j, o], device(z_at(o), y, core),
        )

    def first(j):
        at, wide = out_cuts[j]
        product = jnp.dot(act, down_v[:, at : at + wide], preferred_element_type=F32)
        part[:, at : at + wide] = (product * weight).astype(BF16)
        go(core_copy(j))

    def second(j):
        at, wide = out_cuts[j]
        core_copy(j).wait_recv()
        theirs = core_r[pl.ds(its_y, quarter), at : at + wide].astype(F32)
        here = part[pl.ds(my_half + its_y, quarter), at : at + wide].astype(F32)
        y_s[:, at : at + wide] = (theirs + here).astype(BF16)
        go(y_copy(j))

    def third(j):
        at, wide = out_cuts[j]
        theirs = core_r[pl.ds(my_y, quarter), at : at + wide].astype(F32)
        here = part[pl.ds(my_half + my_y, quarter), at : at + wide].astype(F32)
        y_copy(j).wait_recv()
        total = theirs + here + y_r[:, at : at + wide].astype(F32)
        z_s[:, at : at + wide] = total.astype(BF16)
        for o in range(1, line):
            go(z_copy(j, o))

    def fourth(j):
        at, wide = out_cuts[j]
        total = z_s[pl.ds(my_z, rows), at : at + wide].astype(F32)
        for o in range(1, line):
            z_copy(j, o).wait_recv()
            total = total + z_r[o, :, at : at + wide].astype(F32)
        out_ref[:, at : at + wide] = (
            res_ref[:, at : at + wide].astype(F32) + total
        ).astype(BF16)

    pieces = len(out_cuts)
    for step in range(pieces + 3):
        for lag, stage in enumerate((first, second, third, fourth)):
            if 0 <= step - lag < pieces:
                stage(step - lag)
    for copy in sent:
        copy.wait_send()


def fused(residual, norm_gain, expert_ids, expert_weights, gate_proj, up_proj, down_proj):
    rows, model = residual.shape
    hidden = gate_proj.shape[2]
    devices = lax.axis_size("expert")
    experts = devices // 2
    line = devices // 4
    tokens = rows * devices
    width = -(-(model + 2 * experts) // LANES) * LANES
    in_cuts = cuts(model, 3)
    out_cuts = cuts(model, 3)
    ins, outs = len(in_cuts), len(out_cuts)
    vmem = pl.BlockSpec(memory_space=pltpu.VMEM)
    hbm = pl.BlockSpec(memory_space=pl.ANY)
    dma = pltpu.SemaphoreType.DMA
    return pl.pallas_call(
        functools.partial(kernel, line, experts, in_cuts, out_cuts),
        out_shape=jax.ShapeDtypeStruct((rows, model), BF16),
        in_specs=[vmem] * 4 + [hbm] * 3,
        out_specs=vmem,
        scratch_shapes=[
            pltpu.VMEM((hidden, model), BF16),
            pltpu.VMEM((hidden, model), BF16),
            pltpu.VMEM((hidden, model), BF16),
            pltpu.VMEM((tokens, width), BF16),
            pltpu.VMEM((tokens, hidden), F32),
            pltpu.VMEM((tokens, hidden), F32),
            pltpu.VMEM((tokens, model), BF16),
            pltpu.VMEM((tokens // 2, model), BF16),
            pltpu.VMEM((tokens // 4, model), BF16),
            pltpu.VMEM((tokens // 4, model), BF16),
            pltpu.VMEM((tokens // 4, model), BF16),
            pltpu.VMEM((line, rows, model), BF16),
            dma((ins, 2)),
            dma,
            dma((ins, line)),
            dma((ins, line)),
            dma((ins, line)),
            dma((ins, line)),
            dma((ins, 2)),
            dma((ins, 2)),
            dma((outs,)),
            dma((outs,)),
            dma((outs,)),
            dma((outs,)),
            dma((outs, line)),
            dma((outs, line)),
        ],
        compiler_params=pltpu.CompilerParams(
            collective_id=0, has_side_effects=True, vmem_limit_bytes=60 * 1024 * 1024
        ),
    )(
        residual, norm_gain, expert_ids.T, expert_weights.T,
        gate_proj.transpose(0, 2, 1), up_proj.transpose(0, 2, 1), down_proj,
    )


def body(residual, norm_gain, expert_ids, expert_weights, gate_proj, up_proj, down_proj):
    rows = residual.shape[0]
    devices = lax.axis_size("expert")
    capacity = 4 * rows * expert_ids.shape[1] // devices
    dense = capacity >= rows and devices % 4 == 0
    form = fused if dense else slotted
    return form(
        residual, norm_gain, expert_ids, expert_weights, gate_proj, up_proj, down_proj
    )


def solution(mesh):
    in_specs = (
        P(("groups", "expert"), None),
        P(),
        P(("groups", "expert"), None),
        P(("groups", "expert"), None),
        P("expert", None, None),
        P("expert", None, None),
        P("expert", None, None),
    )
    out_specs = P(("groups", "expert"), None)
    return jax.shard_map(body, mesh=mesh, in_specs=in_specs, out_specs=out_specs, check_vma=False)
```

```python
import functools

import jax
import jax.numpy as jnp
from jax import lax
from jax.experimental import pallas as pl
from jax.experimental.pallas import tpu as pltpu
from jax.sharding import PartitionSpec as P

BF16 = jnp.bfloat16
F32 = jnp.float32
LANES = 128


def partner(value, axis, bit):
    mask = 2**bit
    pairs = [(source, source ^ mask) for source in range(lax.axis_size(axis))]
    return lax.ppermute(value, axis, pairs)


def expert_half(block, gate_w, up_w, down_w):
    flat = block.reshape(-1, block.shape[-1])
    gate = jnp.dot(flat, gate_w, preferred_element_type=jnp.float32)
    upper = jnp.dot(flat, up_w, preferred_element_type=jnp.float32)
    act = (gate * jax.nn.sigmoid(1.702 * gate) * (upper + 1.0)).astype(jnp.bfloat16)
    out = jnp.dot(act, down_w, preferred_element_type=jnp.float32).astype(jnp.bfloat16)
    return out.reshape(block.shape[:-1] + (down_w.shape[1],))


def slotted(residual, norm_gain, expert_ids, expert_weights, gate_proj, up_proj, down_proj):
    rows, model = residual.shape
    chosen = expert_ids.shape[1]
    devices = lax.axis_size("expert")
    experts = devices // 2
    capacity = 2 * rows * chosen // experts
    half_cap = capacity // 2
    gate_w, up_w, down_w = (gate_proj[0], up_proj[0], down_proj[0])
    x = residual.astype(jnp.float32)
    scale = lax.rsqrt(jnp.mean(x * x, axis=-1, keepdims=True) + 1e-05)
    normed = (x * scale * norm_gain).astype(jnp.bfloat16)
    flat_ids = expert_ids.reshape(rows * chosen)
    onehot = (
        flat_ids[:, None] == lax.broadcasted_iota(jnp.int32, (rows * chosen, experts), 1)
    ).astype(jnp.int32)
    slot = jnp.sum(onehot * jnp.cumsum(onehot, axis=0), axis=1) - 1
    position = flat_ids * capacity + slot
    pick = (
        position[:, None] == lax.broadcasted_iota(jnp.int32, (rows * chosen, experts * capacity), 1)
    ).astype(jnp.float32)
    place_rows = jnp.sum(pick.reshape(rows, chosen, experts * capacity), axis=1)
    send = lax.dot_general(
        place_rows.astype(jnp.bfloat16),
        normed,
        (((0,), (0,)), ((), ())),
        preferred_element_type=jnp.float32,
    )
    send = send.astype(jnp.bfloat16).reshape(experts, capacity, model)
    outgoing = send.reshape(experts, 2, half_cap, model).reshape(devices, half_cap, model)
    arrived = lax.all_to_all(outgoing, "expert", split_axis=0, concat_axis=0, tiled=True)
    other = partner(arrived, "expert", 0)
    both = expert_half(jnp.stack((arrived, other)), gate_w, up_w, down_w)
    returned = partner(both[1], "expert", 0)
    finished = (both[0].astype(jnp.float32) + returned.astype(jnp.float32)).astype(jnp.bfloat16)
    back = lax.all_to_all(finished, "expert", split_axis=0, concat_axis=0, tiled=True)
    results = back.reshape(experts, capacity, model)
    weighted = jnp.sum(
        (pick * expert_weights.reshape(rows * chosen)[:, None]).reshape(
            rows, chosen, experts * capacity
        ),
        axis=1,
    )
    combined = jnp.dot(
        weighted,
        results.reshape(experts * capacity, model).astype(jnp.float32),
        precision=lax.Precision.HIGHEST,
    )
    return (x + combined).astype(jnp.bfloat16)


def cuts(total, shares):
    unit = 2 * LANES
    whole = sum(shares)
    ends = [round(total * sum(shares[: n + 1]) / whole / unit) * unit for n in range(len(shares))]
    ends = sorted(set(min(max(e, unit), total) for e in ends[:-1]) | {total})
    starts = [0] + ends[:-1]
    return [(s, e - s) for s, e in zip(starts, ends) if e > s]


def kernel(
    line, experts, in_cuts, out_cuts,
    res_ref, gain_ref, ids_ref, wts_ref, gate_hbm, up_hbm, down_hbm, out_ref,
    gate_v, up_v, down_v, xg, gacc, uacc, part, core_r, y_s, y_r, z_s, z_r,
    w_sem, d_sem, agz_s, agz_r, agy_s, agy_r, agc_s, agc_r,
    rc_s, rc_r, ry_s, ry_r, rz_s, rz_r,
):
    rows, model = res_ref.shape
    extra = xg.shape[1] - model
    halves, short = 1, rows
    tokens = 4 * line * short
    half, quarter = tokens // 2, tokens // 4
    me = lax.axis_index("expert")
    core = lax.rem(me, 2)
    y = lax.rem(me // 2, 2)
    z = me // 4

    def device(z_, y_, c_):
        return (z_ * 2 + y_) * 2 + c_

    def row(h, z_, y_, c_):
        return pl.multiple_of(((c_ * 2 + y_) * line + z_) * short + h * tokens, short)

    def remote(src, dst, send, recv, target):
        return pltpu.make_async_remote_copy(
            src_ref=src, dst_ref=dst, send_sem=send, recv_sem=recv,
            device_id={"expert": target}, device_id_type=pl.DeviceIdType.MESH,
        )

    if line == 4:
        inner = lax.rem((z + 1) // 2, 2)
        beside = z + 1 - 2 * lax.rem(z, 2)
        skip, mirror = lax.rem(z + 2, 4), 3 - z
        others = [
            beside,
            inner * mirror + (1 - inner) * skip,
            inner * skip + (1 - inner) * mirror,
        ]
    else:
        others = [lax.rem(z + o, line) for o in range(1, line)]
    y_dev = device(z, 1 - y, core)
    c_dev = device(z, y, 1 - core)

    loads = []
    for k, (at, wide) in enumerate(in_cuts):
        pair = []
        for n, (hbm, vmem) in enumerate(((gate_hbm, gate_v), (up_hbm, up_v))):
            copy = pltpu.make_async_copy(
                hbm.at[0, :, pl.ds(at, wide)], vmem.at[:, pl.ds(at, wide)], w_sem.at[k, n]
            )
            copy.start()
            pair.append(copy)
        loads.append(pair)
    down_load = pltpu.make_async_copy(down_hbm.at[0], down_v, d_sem)
    down_load.start()

    barrier = pltpu.get_barrier_semaphore()
    peers = [device(z_, y, core) for z_ in others] + [y_dev, c_dev]
    for peer in peers:
        pl.semaphore_signal(
            barrier, inc=1, device_id={"expert": peer}, device_id_type=pl.DeviceIdType.MESH
        )

    x = res_ref[...].astype(F32)
    scale = lax.rsqrt(jnp.mean(x * x, axis=-1, keepdims=True) + 1e-05)
    normed = (x * scale * gain_ref[...]).astype(BF16)
    named = lax.broadcasted_iota(jnp.int32, (extra, rows), 0)
    high = jnp.zeros((extra, rows), F32)
    low = jnp.zeros((extra, rows), F32)
    for k in range(ids_ref.shape[0]):
        ids = ids_ref[k : k + 1, :]
        high = high + jnp.where(ids == named, wts_ref[k : k + 1, :], 0.0)
        low = low + jnp.where(ids + experts == named, wts_ref[k : k + 1, :], 0.0)
    rest = low - low.astype(BF16).astype(F32)
    shares = jnp.transpose(high + rest).astype(BF16)
    for h in range(halves):
        mine = pl.ds(row(h, z, y, core), short)
        xg[mine, 0:model] = normed[h * short : (h + 1) * short]
        xg[mine, model : model + extra] = shares[h * short : (h + 1) * short]

    pl.semaphore_wait(barrier, len(peers))

    sent = []

    def go(copy):
        copy.start()
        sent.append(copy)

    chunks = len(in_cuts)

    def block(k, z_, y_, c_, count):
        at, wide = in_cuts[k]
        if k == chunks - 1:
            wide = wide + extra
        return xg.at[pl.ds(row(0, z_, y_, c_), count * short), pl.ds(at, wide)]

    for k in range(chunks):
        own = block(k, z, y, core, 1)
        go(remote(own, own, agy_s.at[k, z], agy_r.at[k, z], y_dev))
        for there in others:
            go(remote(own, own, agz_s.at[k, there], agz_r.at[k, z], device(there, y, core)))

    def relay_z(h):
        for there in others:
            got = block(h, there, y, core, 1)
            remote(got, got, agz_s.at[h, there], agz_r.at[h, there], c_dev).wait_recv()
            go(remote(got, got, agy_s.at[h, there], agy_r.at[h, there], y_dev))
        group = block(h, 0, y, core, line)
        go(remote(group, group, agc_s.at[h, 0], agc_r.at[h, 0], c_dev))

    def relay_y(h):
        for there in [z] + others:
            got = block(h, there, 1 - y, core, 1)
            remote(got, got, agy_s.at[h, there], agy_r.at[h, there], y_dev).wait_recv()
        group = block(h, 0, 1 - y, core, line)
        go(remote(group, group, agc_s.at[h, 1], agc_r.at[h, 1], c_dev))

    def arrive(h):
        for n, y_ in enumerate((y, 1 - y)):
            group = block(h, 0, y_, 1 - core, line)
            remote(group, group, agc_s.at[h, n], agc_r.at[h, n], c_dev).wait_recv()

    expert = me // 2

    def multiply(k):
        at, wide = in_cuts[k]
        for n, (vmem, acc) in enumerate(((gate_v, gacc), (up_v, uacc))):
            loads[k][n].wait()
            product = lax.dot_general(
                xg[:, at : at + wide], vmem[:, at : at + wide], (((1,), (1,)), ((), ())),
                preferred_element_type=F32,
            )
            if k == 0:
                acc[...] = product
            else:
                acc[...] += product

    def hidden():
        gate = gacc[...]
        act = (gate * jax.nn.sigmoid(1.702 * gate) * (uacc[...] + 1.0)).astype(BF16)
        lanes = lax.broadcasted_iota(jnp.int32, (tokens, extra), 1)
        ours = jnp.logical_or(lanes == expert, lanes == expert + experts)
        weight = jnp.sum(
            jnp.where(ours, xg[:, model : model + extra].astype(F32), 0.0),
            axis=1, keepdims=True,
        )
        return act, weight

    my_half = core * half
    its_half = (1 - core) * half
    my_y = y * quarter
    its_y = (1 - y) * quarter

    def at_row(value, unit):
        return pl.multiple_of(value, unit)

    def core_copy(h, j):
        at, wide = out_cuts[j]
        cols = pl.ds(at, wide)
        return remote(
            part.at[pl.ds(at_row(its_half + h * tokens, half), half), cols],
            core_r.at[pl.ds(h * half, half), cols],
            rc_s.at[h, j], rc_r.at[h, j], c_dev,
        )

    def y_copy(h, j):
        at, wide = out_cuts[j]
        spot = (pl.ds(h * quarter, quarter), pl.ds(at, wide))
        return remote(y_s.at[spot], y_r.at[spot], ry_s.at[h, j], ry_r.at[h, j], y_dev)

    def z_copy(h, j, there):
        at, wide = out_cuts[j]
        cols = pl.ds(at, wide)
        return remote(
            z_s.at[pl.ds(at_row(h * quarter + there * short, short), short), cols],
            z_r.at[pl.ds(at_row(h * quarter + z * short, short), short), cols],
            rz_s.at[h, j, there], rz_r.at[h, j, z], device(there, y, core),
        )

    def z_arrival(h, j, there):
        at, wide = out_cuts[j]
        spot = (pl.ds(at_row(h * quarter + there * short, short), short), pl.ds(at, wide))
        return remote(
            z_r.at[spot], z_r.at[spot], rz_s.at[h, j, there], rz_r.at[h, j, there], c_dev
        )

    def first(h, j, act, weight):
        at, wide = out_cuts[j]
        product = jnp.dot(act, down_v[:, at : at + wide], preferred_element_type=F32)
        part[h * tokens : (h + 1) * tokens, at : at + wide] = (product * weight).astype(BF16)
        go(core_copy(h, j))

    def pair_sum(h, j, which):
        at, wide = out_cuts[j]
        theirs = core_r[pl.ds(at_row(h * half + which, quarter), quarter), at : at + wide]
        here = part[
            pl.ds(at_row(h * tokens + my_half + which, quarter), quarter), at : at + wide
        ]
        return theirs.astype(F32) + here.astype(F32)

    def second(h, j):
        at, wide = out_cuts[j]
        core_copy(h, j).wait_recv()
        y_s[h * quarter : (h + 1) * quarter, at : at + wide] = pair_sum(h, j, its_y).astype(BF16)
        go(y_copy(h, j))

    def third(h, j):
        at, wide = out_cuts[j]
        total = pair_sum(h, j, my_y)
        y_copy(h, j).wait_recv()
        span = slice(h * quarter, (h + 1) * quarter)
        total = total + y_r[span, at : at + wide].astype(F32)
        z_s[span, at : at + wide] = total.astype(BF16)
        for there in others[::-1]:
            go(z_copy(h, j, there))

    def fourth(h, j):
        at, wide = out_cuts[j]
        own = pl.ds(at_row(h * quarter + z * short, short), short)
        total = z_s[own, at : at + wide].astype(F32)
        for there in others:
            z_arrival(h, j, there).wait_recv()
            spot = pl.ds(at_row(h * quarter + there * short, short), short)
            total = total + z_r[spot, at : at + wide].astype(F32)
        span = slice(h * short, (h + 1) * short)
        out_ref[span, at : at + wide] = (
            res_ref[span, at : at + wide].astype(F32) + total
        ).astype(BF16)

    pieces = range(len(out_cuts))
    relay_z(0)
    for k in range(chunks):
        if k + 1 < chunks:
            relay_z(k + 1)
        relay_y(k)
        arrive(k)
        multiply(k)
    act, weight = hidden()
    down_load.wait()
    lags = (0, 1, 3)
    for step in range(len(out_cuts) + lags[-1]):
        for lag, stage in zip(lags, (first, second, third)):
            if 0 <= step - lag < len(out_cuts):
                if stage is first:
                    first(0, step, act, weight)
                else:
                    stage(0, step - lag)
    for h in range(halves):
        for j in pieces:
            fourth(h, j)
    for copy in sent:
        copy.wait_send()


def fused(residual, norm_gain, expert_ids, expert_weights, gate_proj, up_proj, down_proj):
    rows, model = residual.shape
    hidden = gate_proj.shape[2]
    devices = lax.axis_size("expert")
    experts = devices // 2
    line = devices // 4
    halves = 1
    in_cuts = cuts(model, (4, 4, 3))
    ins = len(in_cuts)
    tokens = rows * devices
    width = -(-(model + 2 * experts) // LANES) * LANES
    out_cuts = cuts(model, (2, 3, 3, 2, 1))
    outs = len(out_cuts)
    vmem = pl.BlockSpec(memory_space=pltpu.VMEM)
    hbm = pl.BlockSpec(memory_space=pl.ANY)
    dma = pltpu.SemaphoreType.DMA
    return pl.pallas_call(
        functools.partial(kernel, line, experts, in_cuts, out_cuts),
        out_shape=jax.ShapeDtypeStruct((rows, model), BF16),
        in_specs=[vmem] * 4 + [hbm] * 3,
        out_specs=vmem,
        scratch_shapes=[
            pltpu.VMEM((hidden, model), BF16),
            pltpu.VMEM((hidden, model), BF16),
            pltpu.VMEM((hidden, model), BF16),
            pltpu.VMEM((tokens, width), BF16),
            pltpu.VMEM((tokens, hidden), F32),
            pltpu.VMEM((tokens, hidden), F32),
            pltpu.VMEM((tokens, model), BF16),
            pltpu.VMEM((tokens // 2, model), BF16),
            pltpu.VMEM((tokens // 4, model), BF16),
            pltpu.VMEM((tokens // 4, model), BF16),
            pltpu.VMEM((tokens // 4, model), BF16),
            pltpu.VMEM((tokens // 4, model), BF16),
            dma((ins, 2)),
            dma,
            dma((ins, line)),
            dma((ins, line)),
            dma((ins, line)),
            dma((ins, line)),
            dma((ins, 2)),
            dma((ins, 2)),
            dma((halves, outs)),
            dma((halves, outs)),
            dma((halves, outs)),
            dma((halves, outs)),
            dma((halves, outs, line)),
            dma((halves, outs, line)),
        ],
        compiler_params=pltpu.CompilerParams(
            collective_id=0, has_side_effects=True, vmem_limit_bytes=60 * 1024 * 1024
        ),
    )(
        residual, norm_gain, expert_ids.T, expert_weights.T,
        gate_proj.transpose(0, 2, 1), up_proj.transpose(0, 2, 1), down_proj,
    )


def body(residual, norm_gain, expert_ids, expert_weights, gate_proj, up_proj, down_proj):
    rows = residual.shape[0]
    devices = lax.axis_size("expert")
    capacity = 4 * rows * expert_ids.shape[1] // devices
    dense = capacity >= rows and devices % 4 == 0
    form = fused if dense else slotted
    return form(
        residual, norm_gain, expert_ids, expert_weights, gate_proj, up_proj, down_proj
    )


def solution(mesh):
    in_specs = (
        P(("groups", "expert"), None),
        P(),
        P(("groups", "expert"), None),
        P(("groups", "expert"), None),
        P("expert", None, None),
        P("expert", None, None),
        P("expert", None, None),
    )
    out_specs = P(("groups", "expert"), None)
    return jax.shard_map(body, mesh=mesh, in_specs=in_specs, out_specs=out_specs, check_vma=False)
```

```python
import functools

import jax
import jax.numpy as jnp
from jax import lax
from jax.experimental import pallas as pl
from jax.experimental.pallas import tpu as pltpu
from jax.sharding import PartitionSpec as P

BF16 = jnp.bfloat16
F32 = jnp.float32
LANES = 128


def partner(value, axis, bit):
    mask = 2**bit
    pairs = [(source, source ^ mask) for source in range(lax.axis_size(axis))]
    return lax.ppermute(value, axis, pairs)


def expert_half(block, gate_w, up_w, down_w):
    flat = block.reshape(-1, block.shape[-1])
    gate = jnp.dot(flat, gate_w, preferred_element_type=jnp.float32)
    upper = jnp.dot(flat, up_w, preferred_element_type=jnp.float32)
    act = (gate * jax.nn.sigmoid(1.702 * gate) * (upper + 1.0)).astype(jnp.bfloat16)
    out = jnp.dot(act, down_w, preferred_element_type=jnp.float32).astype(jnp.bfloat16)
    return out.reshape(block.shape[:-1] + (down_w.shape[1],))


def slotted(residual, norm_gain, expert_ids, expert_weights, gate_proj, up_proj, down_proj):
    rows, model = residual.shape
    chosen = expert_ids.shape[1]
    devices = lax.axis_size("expert")
    experts = devices // 2
    capacity = 2 * rows * chosen // experts
    half_cap = capacity // 2
    gate_w, up_w, down_w = (gate_proj[0], up_proj[0], down_proj[0])
    x = residual.astype(jnp.float32)
    scale = lax.rsqrt(jnp.mean(x * x, axis=-1, keepdims=True) + 1e-05)
    normed = (x * scale * norm_gain).astype(jnp.bfloat16)
    flat_ids = expert_ids.reshape(rows * chosen)
    onehot = (
        flat_ids[:, None] == lax.broadcasted_iota(jnp.int32, (rows * chosen, experts), 1)
    ).astype(jnp.int32)
    slot = jnp.sum(onehot * jnp.cumsum(onehot, axis=0), axis=1) - 1
    position = flat_ids * capacity + slot
    pick = (
        position[:, None] == lax.broadcasted_iota(jnp.int32, (rows * chosen, experts * capacity), 1)
    ).astype(jnp.float32)
    place_rows = jnp.sum(pick.reshape(rows, chosen, experts * capacity), axis=1)
    send = lax.dot_general(
        place_rows.astype(jnp.bfloat16),
        normed,
        (((0,), (0,)), ((), ())),
        preferred_element_type=jnp.float32,
    )
    send = send.astype(jnp.bfloat16).reshape(experts, capacity, model)
    outgoing = send.reshape(experts, 2, half_cap, model).reshape(devices, half_cap, model)
    arrived = lax.all_to_all(outgoing, "expert", split_axis=0, concat_axis=0, tiled=True)
    other = partner(arrived, "expert", 0)
    both = expert_half(jnp.stack((arrived, other)), gate_w, up_w, down_w)
    returned = partner(both[1], "expert", 0)
    finished = (both[0].astype(jnp.float32) + returned.astype(jnp.float32)).astype(jnp.bfloat16)
    back = lax.all_to_all(finished, "expert", split_axis=0, concat_axis=0, tiled=True)
    results = back.reshape(experts, capacity, model)
    weighted = jnp.sum(
        (pick * expert_weights.reshape(rows * chosen)[:, None]).reshape(
            rows, chosen, experts * capacity
        ),
        axis=1,
    )
    combined = jnp.dot(
        weighted,
        results.reshape(experts * capacity, model).astype(jnp.float32),
        precision=lax.Precision.HIGHEST,
    )
    return (x + combined).astype(jnp.bfloat16)


def cuts(total, shares):
    unit = 2 * LANES
    whole = sum(shares)
    ends = [round(total * sum(shares[: n + 1]) / whole / unit) * unit for n in range(len(shares))]
    ends = sorted(set(min(max(e, unit), total) for e in ends[:-1]) | {total})
    starts = [0] + ends[:-1]
    return [(s, e - s) for s, e in zip(starts, ends) if e > s]


def kernel(
    line, experts, in_cuts, out_cuts,
    res_ref, gain_ref, ids_ref, wts_ref, gate_hbm, up_hbm, down_hbm, out_ref,
    gate_v, up_v, down_v, xg, gacc, uacc, part, core_r, y_s, y_r, z_s, z_r,
    w_sem, d_sem, agl_s, agr_s, agz_r, agy_s, agy_r, agc_s, agc_r,
    rc_s, rc_r, ry_s, ry_r, rz_s, rz_r,
):
    rows, model = res_ref.shape
    extra = xg.shape[1] - model
    halves, short = 1, rows
    tokens = 4 * line * short
    half, quarter = tokens // 2, tokens // 4
    me = lax.axis_index("expert")
    core = lax.rem(me, 2)
    y = lax.rem(me // 2, 2)
    z = me // 4

    def device(z_, y_, c_):
        return (z_ * 2 + y_) * 2 + c_

    def row(h, z_, y_, c_):
        return pl.multiple_of(((c_ * 2 + y_) * line + z_) * short + h * tokens, short)

    def remote(src, dst, send, recv, target):
        return pltpu.make_async_remote_copy(
            src_ref=src, dst_ref=dst, send_sem=send, recv_sem=recv,
            device_id={"expert": target}, device_id_type=pl.DeviceIdType.MESH,
        )

    if line == 4:
        inner = lax.rem((z + 1) // 2, 2)
        beside = z + 1 - 2 * lax.rem(z, 2)
        skip, mirror = lax.rem(z + 2, 4), 3 - z
        others = [
            beside,
            inner * mirror + (1 - inner) * skip,
            inner * skip + (1 - inner) * mirror,
        ]
    else:
        others = [lax.rem(z + o, line) for o in range(1, line)]
    y_dev = device(z, 1 - y, core)
    c_dev = device(z, y, 1 - core)

    loads = []
    for k, (at, wide) in enumerate(in_cuts):
        pair = []
        for n, (hbm, vmem) in enumerate(((gate_hbm, gate_v), (up_hbm, up_v))):
            copy = pltpu.make_async_copy(
                hbm.at[0, :, pl.ds(at, wide)], vmem.at[:, pl.ds(at, wide)], w_sem.at[k, n]
            )
            copy.start()
            pair.append(copy)
        loads.append(pair)
    down_load = pltpu.make_async_copy(down_hbm.at[0], down_v, d_sem)
    down_load.start()

    barrier = pltpu.get_barrier_semaphore()
    last = line - 1
    has_left = (z + last) // line
    has_right = (2 * last - z) // line

    def greet(peer):
        pl.semaphore_signal(
            barrier, inc=1, device_id={"expert": peer}, device_id_type=pl.DeviceIdType.MESH
        )

    greet(y_dev)
    greet(c_dev)
    pl.when(z > 0)(lambda: greet(device(z - 1, y, core)))
    pl.when(z < last)(lambda: greet(device(z + 1, y, core)))

    x = res_ref[...].astype(F32)
    scale = lax.rsqrt(jnp.mean(x * x, axis=-1, keepdims=True) + 1e-05)
    normed = (x * scale * gain_ref[...]).astype(BF16)
    named = lax.broadcasted_iota(jnp.int32, (extra, rows), 0)
    high = jnp.zeros((extra, rows), F32)
    low = jnp.zeros((extra, rows), F32)
    for k in range(ids_ref.shape[0]):
        ids = ids_ref[k : k + 1, :]
        high = high + jnp.where(ids == named, wts_ref[k : k + 1, :], 0.0)
        low = low + jnp.where(ids + experts == named, wts_ref[k : k + 1, :], 0.0)
    rest = low - low.astype(BF16).astype(F32)
    shares = jnp.transpose(high + rest).astype(BF16)
    for h in range(halves):
        mine = pl.ds(row(h, z, y, core), short)
        xg[mine, 0:model] = normed[h * short : (h + 1) * short]
        xg[mine, model : model + extra] = shares[h * short : (h + 1) * short]

    pl.semaphore_wait(barrier, 2 + has_left + has_right)

    sent = []

    def go(copy):
        copy.start()
        sent.append(copy)

    chunks = len(in_cuts)

    def block(k, z_, y_, c_, count):
        at, wide = in_cuts[k]
        if k == chunks - 1:
            wide = wide + extra
        return xg.at[pl.ds(row(0, z_, y_, c_), count * short), pl.ds(at, wide)]

    def pass_left(k, z_):
        at = block(k, z_, y, core, 1)
        return remote(at, at, agl_s.at[k, z_], agz_r.at[k, z_], device(z - 1, y, core))

    def pass_right(k, z_):
        at = block(k, z_, y, core, 1)
        return remote(at, at, agr_s.at[k, z_], agz_r.at[k, z_], device(z + 1, y, core))

    def pass_y(k, z_):
        at = block(k, z_, y, core, 1)
        return remote(at, at, agy_s.at[k, z_], agy_r.at[k, z_], y_dev)

    def from_right(k, d):
        pass_left(k, z + d).wait_recv()
        pass_y(k, z + d).start()
        pl.when(z > 0)(lambda: pass_left(k, z + d).start())

    def from_left(k, d):
        pass_right(k, z - d).wait_recv()
        pass_y(k, z - d).start()
        pl.when(z < last)(lambda: pass_right(k, z - d).start())

    for k in range(chunks):
        pass_y(k, z).start()
        pl.when(z > 0)(lambda: pass_left(k, z).start())
        pl.when(z < last)(lambda: pass_right(k, z).start())

    def line_step(d, k):
        pl.when(z + d <= last)(lambda: from_right(k, d))
        pl.when(z - d >= 0)(lambda: from_left(k, d))

    def core_group(k, n):
        group = block(k, 0, y if n == 0 else 1 - y, core, line)
        go(remote(group, group, agc_s.at[k, n], agc_r.at[k, n], c_dev))

    def relay_y(k):
        for there in range(line):
            got = block(k, there, 1 - y, core, 1)
            remote(got, got, agy_s.at[k, there], agy_r.at[k, there], y_dev).wait_recv()
        core_group(k, 1)

    def arrive(k):
        for n, y_ in enumerate((y, 1 - y)):
            group = block(k, 0, y_, 1 - core, line)
            remote(group, group, agc_s.at[k, n], agc_r.at[k, n], c_dev).wait_recv()

    def drain_gather():
        for k in range(chunks):
            for z_ in range(line):
                pass_y(k, z_).wait_send()
                pl.when(jnp.logical_and(z > 0, z <= z_))(
                    lambda: pass_left(k, z_).wait_send()
                )
                pl.when(jnp.logical_and(z < last, z >= z_))(
                    lambda: pass_right(k, z_).wait_send()
                )

    expert = me // 2

    def multiply(k):
        at, wide = in_cuts[k]
        for n, (vmem, acc) in enumerate(((gate_v, gacc), (up_v, uacc))):
            loads[k][n].wait()
            product = lax.dot_general(
                xg[:, at : at + wide], vmem[:, at : at + wide], (((1,), (1,)), ((), ())),
                preferred_element_type=F32,
            )
            if k == 0:
                acc[...] = product
            else:
                acc[...] += product

    def hidden():
        gate = gacc[...]
        act = (gate * jax.nn.sigmoid(1.702 * gate) * (uacc[...] + 1.0)).astype(BF16)
        lanes = lax.broadcasted_iota(jnp.int32, (tokens, extra), 1)
        ours = jnp.logical_or(lanes == expert, lanes == expert + experts)
        weight = jnp.sum(
            jnp.where(ours, xg[:, model : model + extra].astype(F32), 0.0),
            axis=1, keepdims=True,
        )
        return act, weight

    my_half = core * half
    its_half = (1 - core) * half
    my_y = y * quarter
    its_y = (1 - y) * quarter

    def at_row(value, unit):
        return pl.multiple_of(value, unit)

    def core_copy(h, j):
        at, wide = out_cuts[j]
        cols = pl.ds(at, wide)
        return remote(
            part.at[pl.ds(at_row(its_half + h * tokens, half), half), cols],
            core_r.at[pl.ds(h * half, half), cols],
            rc_s.at[h, j], rc_r.at[h, j], c_dev,
        )

    def y_copy(h, j):
        at, wide = out_cuts[j]
        spot = (pl.ds(h * quarter, quarter), pl.ds(at, wide))
        return remote(y_s.at[spot], y_r.at[spot], ry_s.at[h, j], ry_r.at[h, j], y_dev)

    def z_copy(h, j, there):
        at, wide = out_cuts[j]
        cols = pl.ds(at, wide)
        return remote(
            z_s.at[pl.ds(at_row(h * quarter + there * short, short), short), cols],
            z_r.at[pl.ds(at_row(h * quarter + z * short, short), short), cols],
            rz_s.at[h, j, there], rz_r.at[h, j, z], device(there, y, core),
        )

    def z_arrival(h, j, there):
        at, wide = out_cuts[j]
        spot = (pl.ds(at_row(h * quarter + there * short, short), short), pl.ds(at, wide))
        return remote(
            z_r.at[spot], z_r.at[spot], rz_s.at[h, j, there], rz_r.at[h, j, there], c_dev
        )

    def first(h, j, act, weight):
        at, wide = out_cuts[j]
        product = jnp.dot(act, down_v[:, at : at + wide], preferred_element_type=F32)
        part[h * tokens : (h + 1) * tokens, at : at + wide] = (product * weight).astype(BF16)
        go(core_copy(h, j))

    def pair_sum(h, j, which):
        at, wide = out_cuts[j]
        theirs = core_r[pl.ds(at_row(h * half + which, quarter), quarter), at : at + wide]
        here = part[
            pl.ds(at_row(h * tokens + my_half + which, quarter), quarter), at : at + wide
        ]
        return theirs.astype(F32) + here.astype(F32)

    def second(h, j):
        at, wide = out_cuts[j]
        core_copy(h, j).wait_recv()
        y_s[h * quarter : (h + 1) * quarter, at : at + wide] = pair_sum(h, j, its_y).astype(BF16)
        go(y_copy(h, j))

    def third(h, j):
        at, wide = out_cuts[j]
        total = pair_sum(h, j, my_y)
        y_copy(h, j).wait_recv()
        span = slice(h * quarter, (h + 1) * quarter)
        total = total + y_r[span, at : at + wide].astype(F32)
        z_s[span, at : at + wide] = total.astype(BF16)
        for there in others[::-1]:
            go(z_copy(h, j, there))

    def fourth(h, j):
        at, wide = out_cuts[j]
        own = pl.ds(at_row(h * quarter + z * short, short), short)
        total = z_s[own, at : at + wide].astype(F32)
        for there in others:
            z_arrival(h, j, there).wait_recv()
            spot = pl.ds(at_row(h * quarter + there * short, short), short)
            total = total + z_r[spot, at : at + wide].astype(F32)
        span = slice(h * short, (h + 1) * short)
        out_ref[span, at : at + wide] = (
            res_ref[span, at : at + wide].astype(F32) + total
        ).astype(BF16)

    pieces = range(len(out_cuts))
    for d in range(1, line):
        for k in range(chunks):
            line_step(d, k)
            if d == last:
                core_group(k, 0)
    for k in range(chunks):
        relay_y(k)
    for k in range(chunks):
        arrive(k)
        multiply(k)
    act, weight = hidden()
    down_load.wait()
    lags = (0, 1, 3)
    for step in range(len(out_cuts) + lags[-1]):
        for lag, stage in zip(lags, (first, second, third)):
            if 0 <= step - lag < len(out_cuts):
                if stage is first:
                    first(0, step, act, weight)
                else:
                    stage(0, step - lag)
    for h in range(halves):
        for j in pieces:
            fourth(h, j)
    drain_gather()
    for copy in sent:
        copy.wait_send()


def fused(residual, norm_gain, expert_ids, expert_weights, gate_proj, up_proj, down_proj):
    rows, model = residual.shape
    hidden = gate_proj.shape[2]
    devices = lax.axis_size("expert")
    experts = devices // 2
    line = devices // 4
    halves = 1
    in_cuts = cuts(model, (4, 4, 3))
    ins = len(in_cuts)
    tokens = rows * devices
    width = -(-(model + 2 * experts) // LANES) * LANES
    out_cuts = cuts(model, (2, 3, 3, 2, 1))
    outs = len(out_cuts)
    vmem = pl.BlockSpec(memory_space=pltpu.VMEM)
    hbm = pl.BlockSpec(memory_space=pl.ANY)
    dma = pltpu.SemaphoreType.DMA
    return pl.pallas_call(
        functools.partial(kernel, line, experts, in_cuts, out_cuts),
        out_shape=jax.ShapeDtypeStruct((rows, model), BF16),
        in_specs=[vmem] * 4 + [hbm] * 3,
        out_specs=vmem,
        scratch_shapes=[
            pltpu.VMEM((hidden, model), BF16),
            pltpu.VMEM((hidden, model), BF16),
            pltpu.VMEM((hidden, model), BF16),
            pltpu.VMEM((tokens, width), BF16),
            pltpu.VMEM((tokens, hidden), F32),
            pltpu.VMEM((tokens, hidden), F32),
            pltpu.VMEM((tokens, model), BF16),
            pltpu.VMEM((tokens // 2, model), BF16),
            pltpu.VMEM((tokens // 4, model), BF16),
            pltpu.VMEM((tokens // 4, model), BF16),
            pltpu.VMEM((tokens // 4, model), BF16),
            pltpu.VMEM((tokens // 4, model), BF16),
            dma((ins, 2)),
            dma,
            dma((ins, line)),
            dma((ins, line)),
            dma((ins, line)),
            dma((ins, line)),
            dma((ins, line)),
            dma((ins, 2)),
            dma((ins, 2)),
            dma((halves, outs)),
            dma((halves, outs)),
            dma((halves, outs)),
            dma((halves, outs)),
            dma((halves, outs, line)),
            dma((halves, outs, line)),
        ],
        compiler_params=pltpu.CompilerParams(
            collective_id=0, has_side_effects=True, vmem_limit_bytes=60 * 1024 * 1024
        ),
    )(
        residual, norm_gain, expert_ids.T, expert_weights.T,
        gate_proj.transpose(0, 2, 1), up_proj.transpose(0, 2, 1), down_proj,
    )


def body(residual, norm_gain, expert_ids, expert_weights, gate_proj, up_proj, down_proj):
    rows = residual.shape[0]
    devices = lax.axis_size("expert")
    capacity = 4 * rows * expert_ids.shape[1] // devices
    dense = capacity >= rows and devices % 4 == 0
    form = fused if dense else slotted
    return form(
        residual, norm_gain, expert_ids, expert_weights, gate_proj, up_proj, down_proj
    )


def solution(mesh):
    in_specs = (
        P(("groups", "expert"), None),
        P(),
        P(("groups", "expert"), None),
        P(("groups", "expert"), None),
        P("expert", None, None),
        P("expert", None, None),
        P("expert", None, None),
    )
    out_specs = P(("groups", "expert"), None)
    return jax.shard_map(body, mesh=mesh, in_specs=in_specs, out_specs=out_specs, check_vma=False)
```

```python
import functools

import jax
import jax.numpy as jnp
from jax import lax
from jax.experimental import pallas as pl
from jax.experimental.pallas import tpu as pltpu
from jax.sharding import PartitionSpec as P

BF16 = jnp.bfloat16
F32 = jnp.float32
LANES = 128


def partner(value, axis, bit):
    mask = 2**bit
    pairs = [(source, source ^ mask) for source in range(lax.axis_size(axis))]
    return lax.ppermute(value, axis, pairs)


def expert_half(block, gate_w, up_w, down_w):
    flat = block.reshape(-1, block.shape[-1])
    gate = jnp.dot(flat, gate_w, preferred_element_type=jnp.float32)
    upper = jnp.dot(flat, up_w, preferred_element_type=jnp.float32)
    act = (gate * jax.nn.sigmoid(1.702 * gate) * (upper + 1.0)).astype(jnp.bfloat16)
    out = jnp.dot(act, down_w, preferred_element_type=jnp.float32).astype(jnp.bfloat16)
    return out.reshape(block.shape[:-1] + (down_w.shape[1],))


def slotted(residual, norm_gain, expert_ids, expert_weights, gate_proj, up_proj, down_proj):
    rows, model = residual.shape
    chosen = expert_ids.shape[1]
    devices = lax.axis_size("expert")
    experts = devices // 2
    capacity = 2 * rows * chosen // experts
    half_cap = capacity // 2
    gate_w, up_w, down_w = (gate_proj[0], up_proj[0], down_proj[0])
    x = residual.astype(jnp.float32)
    scale = lax.rsqrt(jnp.mean(x * x, axis=-1, keepdims=True) + 1e-05)
    normed = (x * scale * norm_gain).astype(jnp.bfloat16)
    flat_ids = expert_ids.reshape(rows * chosen)
    onehot = (
        flat_ids[:, None] == lax.broadcasted_iota(jnp.int32, (rows * chosen, experts), 1)
    ).astype(jnp.int32)
    slot = jnp.sum(onehot * jnp.cumsum(onehot, axis=0), axis=1) - 1
    position = flat_ids * capacity + slot
    pick = (
        position[:, None] == lax.broadcasted_iota(jnp.int32, (rows * chosen, experts * capacity), 1)
    ).astype(jnp.float32)
    place_rows = jnp.sum(pick.reshape(rows, chosen, experts * capacity), axis=1)
    send = lax.dot_general(
        place_rows.astype(jnp.bfloat16),
        normed,
        (((0,), (0,)), ((), ())),
        preferred_element_type=jnp.float32,
    )
    send = send.astype(jnp.bfloat16).reshape(experts, capacity, model)
    outgoing = send.reshape(experts, 2, half_cap, model).reshape(devices, half_cap, model)
    arrived = lax.all_to_all(outgoing, "expert", split_axis=0, concat_axis=0, tiled=True)
    other = partner(arrived, "expert", 0)
    both = expert_half(jnp.stack((arrived, other)), gate_w, up_w, down_w)
    returned = partner(both[1], "expert", 0)
    finished = (both[0].astype(jnp.float32) + returned.astype(jnp.float32)).astype(jnp.bfloat16)
    back = lax.all_to_all(finished, "expert", split_axis=0, concat_axis=0, tiled=True)
    results = back.reshape(experts, capacity, model)
    weighted = jnp.sum(
        (pick * expert_weights.reshape(rows * chosen)[:, None]).reshape(
            rows, chosen, experts * capacity
        ),
        axis=1,
    )
    combined = jnp.dot(
        weighted,
        results.reshape(experts * capacity, model).astype(jnp.float32),
        precision=lax.Precision.HIGHEST,
    )
    return (x + combined).astype(jnp.bfloat16)


def cuts(total, shares):
    unit = 2 * LANES
    whole = sum(shares)
    ends = [round(total * sum(shares[: n + 1]) / whole / unit) * unit for n in range(len(shares))]
    ends = sorted(set(min(max(e, unit), total) for e in ends[:-1]) | {total})
    starts = [0] + ends[:-1]
    return [(s, e - s) for s, e in zip(starts, ends) if e > s]


def kernel(
    line, experts, in_cuts, out_cuts,
    res_ref, gain_ref, ids_ref, wts_ref, gate_hbm, up_hbm, down_hbm, out_ref,
    gate_v, up_v, down_v, xg, gacc, uacc, part, core_r, y_s, y_r, z_s, z_r,
    w_sem, d_sem, agl_s, agr_s, agz_r, agy_s, agy_r, agc_s, agc_r,
    rc_s, rc_r, ry_s, ry_r, rz_s, rz_r,
):
    rows, model = res_ref.shape
    extra = xg.shape[1] - model
    halves, short = 1, rows
    tokens = 4 * line * short
    half, quarter = tokens // 2, tokens // 4
    me = lax.axis_index("expert")
    core = lax.rem(me, 2)
    y = lax.rem(me // 2, 2)
    z = me // 4

    def device(z_, y_, c_):
        return (z_ * 2 + y_) * 2 + c_

    def row(h, z_, y_, c_):
        return pl.multiple_of(((c_ * 2 + y_) * line + z_) * short + h * tokens, short)

    def remote(src, dst, send, recv, target):
        return pltpu.make_async_remote_copy(
            src_ref=src, dst_ref=dst, send_sem=send, recv_sem=recv,
            device_id={"expert": target}, device_id_type=pl.DeviceIdType.MESH,
        )

    if line == 4:
        inner = lax.rem((z + 1) // 2, 2)
        beside = z + 1 - 2 * lax.rem(z, 2)
        skip, mirror = lax.rem(z + 2, 4), 3 - z
        others = [
            beside,
            inner * mirror + (1 - inner) * skip,
            inner * skip + (1 - inner) * mirror,
        ]
    else:
        others = [lax.rem(z + o, line) for o in range(1, line)]
    y_dev = device(z, 1 - y, core)
    c_dev = device(z, y, 1 - core)

    loads = []
    for k, (at, wide) in enumerate(in_cuts):
        pair = []
        for n, (hbm, vmem) in enumerate(((gate_hbm, gate_v), (up_hbm, up_v))):
            copy = pltpu.make_async_copy(
                hbm.at[0, :, pl.ds(at, wide)], vmem.at[:, pl.ds(at, wide)], w_sem.at[k, n]
            )
            copy.start()
            pair.append(copy)
        loads.append(pair)
    down_load = pltpu.make_async_copy(down_hbm.at[0], down_v, d_sem)
    down_load.start()

    barrier = pltpu.get_barrier_semaphore()
    last = line - 1
    has_left = (z + last) // line
    has_right = (2 * last - z) // line

    def greet(peer):
        pl.semaphore_signal(
            barrier, inc=1, device_id={"expert": peer}, device_id_type=pl.DeviceIdType.MESH
        )

    greet(y_dev)
    greet(c_dev)
    pl.when(z > 0)(lambda: greet(device(z - 1, y, core)))
    pl.when(z < last)(lambda: greet(device(z + 1, y, core)))

    x = res_ref[...].astype(F32)
    scale = lax.rsqrt(jnp.mean(x * x, axis=-1, keepdims=True) + 1e-05)
    normed = (x * scale * gain_ref[...]).astype(BF16)
    named = lax.broadcasted_iota(jnp.int32, (extra, rows), 0)
    high = jnp.zeros((extra, rows), F32)
    low = jnp.zeros((extra, rows), F32)
    for k in range(ids_ref.shape[0]):
        ids = ids_ref[k : k + 1, :]
        high = high + jnp.where(ids == named, wts_ref[k : k + 1, :], 0.0)
        low = low + jnp.where(ids + experts == named, wts_ref[k : k + 1, :], 0.0)
    rest = low - low.astype(BF16).astype(F32)
    shares = jnp.transpose(high + rest).astype(BF16)
    for h in range(halves):
        mine = pl.ds(row(h, z, y, core), short)
        xg[mine, 0:model] = normed[h * short : (h + 1) * short]
        xg[mine, model : model + extra] = shares[h * short : (h + 1) * short]

    pl.semaphore_wait(barrier, 2 + has_left + has_right)

    sent = []

    def go(copy):
        copy.start()
        sent.append(copy)

    chunks = len(in_cuts)

    def block(k, z_, y_, c_, count):
        at, wide = in_cuts[k]
        if k == chunks - 1:
            wide = wide + extra
        return xg.at[pl.ds(row(0, z_, y_, c_), count * short), pl.ds(at, wide)]

    def pass_left(k, z_):
        at = block(k, z_, y, core, 1)
        return remote(at, at, agl_s.at[k, z_], agz_r.at[k, z_], device(z - 1, y, core))

    def pass_right(k, z_):
        at = block(k, z_, y, core, 1)
        return remote(at, at, agr_s.at[k, z_], agz_r.at[k, z_], device(z + 1, y, core))

    def pass_y(k, z_):
        at = block(k, z_, y, core, 1)
        return remote(at, at, agy_s.at[k, z_], agy_r.at[k, z_], y_dev)

    def from_right(k, d):
        pass_left(k, z + d).wait_recv()
        pass_y(k, z + d).start()
        pl.when(z > 0)(lambda: pass_left(k, z + d).start())

    def from_left(k, d):
        pass_right(k, z - d).wait_recv()
        pass_y(k, z - d).start()
        pl.when(z < last)(lambda: pass_right(k, z - d).start())

    for k in range(chunks):
        pass_y(k, z).start()
        pl.when(z > 0)(lambda: pass_left(k, z).start())
        pl.when(z < last)(lambda: pass_right(k, z).start())

    def line_step(d, k):
        pl.when(z + d <= last)(lambda: from_right(k, d))
        pl.when(z - d >= 0)(lambda: from_left(k, d))

    def core_group(k, n):
        group = block(k, 0, y if n == 0 else 1 - y, core, line)
        go(remote(group, group, agc_s.at[k, n], agc_r.at[k, n], c_dev))

    def relay_y(k):
        for there in range(line):
            got = block(k, there, 1 - y, core, 1)
            remote(got, got, agy_s.at[k, there], agy_r.at[k, there], y_dev).wait_recv()
        core_group(k, 1)

    def arrive(k):
        for n, y_ in enumerate((y, 1 - y)):
            group = block(k, 0, y_, 1 - core, line)
            remote(group, group, agc_s.at[k, n], agc_r.at[k, n], c_dev).wait_recv()

    def drain_gather():
        for k in range(chunks):
            for z_ in range(line):
                pass_y(k, z_).wait_send()
                pl.when(jnp.logical_and(z > 0, z <= z_))(
                    lambda: pass_left(k, z_).wait_send()
                )
                pl.when(jnp.logical_and(z < last, z >= z_))(
                    lambda: pass_right(k, z_).wait_send()
                )

    expert = me // 2

    def multiply(k):
        at, wide = in_cuts[k]
        for n, (vmem, acc) in enumerate(((gate_v, gacc), (up_v, uacc))):
            loads[k][n].wait()
            product = lax.dot_general(
                xg[:, at : at + wide], vmem[:, at : at + wide], (((1,), (1,)), ((), ())),
                preferred_element_type=F32,
            )
            if k == 0:
                acc[...] = product
            else:
                acc[...] += product

    def hidden():
        gate = gacc[...]
        act = (gate * jax.nn.sigmoid(1.702 * gate) * (uacc[...] + 1.0)).astype(BF16)
        lanes = lax.broadcasted_iota(jnp.int32, (tokens, extra), 1)
        ours = jnp.logical_or(lanes == expert, lanes == expert + experts)
        weight = jnp.sum(
            jnp.where(ours, xg[:, model : model + extra].astype(F32), 0.0),
            axis=1, keepdims=True,
        )
        return act, weight

    my_half = core * half
    its_half = (1 - core) * half
    my_y = y * quarter
    its_y = (1 - y) * quarter

    def at_row(value, unit):
        return pl.multiple_of(value, unit)

    def core_copy(h, j):
        at, wide = out_cuts[j]
        cols = pl.ds(at, wide)
        return remote(
            part.at[pl.ds(at_row(its_half + h * tokens, half), half), cols],
            core_r.at[pl.ds(h * half, half), cols],
            rc_s.at[h, j], rc_r.at[h, j], c_dev,
        )

    def y_copy(h, j):
        at, wide = out_cuts[j]
        spot = (pl.ds(h * quarter, quarter), pl.ds(at, wide))
        return remote(y_s.at[spot], y_r.at[spot], ry_s.at[h, j], ry_r.at[h, j], y_dev)

    def z_copy(h, j, there):
        at, wide = out_cuts[j]
        cols = pl.ds(at, wide)
        return remote(
            z_s.at[pl.ds(at_row(h * quarter + there * short, short), short), cols],
            z_r.at[pl.ds(at_row(h * quarter + z * short, short), short), cols],
            rz_s.at[h, j, there], rz_r.at[h, j, z], device(there, y, core),
        )

    def z_arrival(h, j, there):
        at, wide = out_cuts[j]
        spot = (pl.ds(at_row(h * quarter + there * short, short), short), pl.ds(at, wide))
        return remote(
            z_r.at[spot], z_r.at[spot], rz_s.at[h, j, there], rz_r.at[h, j, there], c_dev
        )

    def first(h, j, act, weight):
        at, wide = out_cuts[j]
        product = jnp.dot(act, down_v[:, at : at + wide], preferred_element_type=F32)
        part[h * tokens : (h + 1) * tokens, at : at + wide] = (product * weight).astype(BF16)
        go(core_copy(h, j))

    def pair_sum(h, j, which):
        at, wide = out_cuts[j]
        theirs = core_r[pl.ds(at_row(h * half + which, quarter), quarter), at : at + wide]
        here = part[
            pl.ds(at_row(h * tokens + my_half + which, quarter), quarter), at : at + wide
        ]
        return theirs.astype(F32) + here.astype(F32)

    def second(h, j):
        at, wide = out_cuts[j]
        core_copy(h, j).wait_recv()
        y_s[h * quarter : (h + 1) * quarter, at : at + wide] = pair_sum(h, j, its_y).astype(BF16)
        go(y_copy(h, j))

    def third(h, j):
        at, wide = out_cuts[j]
        total = pair_sum(h, j, my_y)
        y_copy(h, j).wait_recv()
        span = slice(h * quarter, (h + 1) * quarter)
        total = total + y_r[span, at : at + wide].astype(F32)
        z_s[span, at : at + wide] = total.astype(BF16)
        for there in others[::-1]:
            go(z_copy(h, j, there))

    def fourth(h, j):
        at, wide = out_cuts[j]
        own = pl.ds(at_row(h * quarter + z * short, short), short)
        total = z_s[own, at : at + wide].astype(F32)
        for there in others:
            z_arrival(h, j, there).wait_recv()
            spot = pl.ds(at_row(h * quarter + there * short, short), short)
            total = total + z_r[spot, at : at + wide].astype(F32)
        span = slice(h * short, (h + 1) * short)
        out_ref[span, at : at + wide] = (
            res_ref[span, at : at + wide].astype(F32) + total
        ).astype(BF16)

    pieces = range(len(out_cuts))
    for d in range(1, line):
        for k in range(chunks):
            line_step(d, k)
            if d == last:
                core_group(k, 0)
    for k in range(chunks):
        relay_y(k)
    for k in range(chunks):
        arrive(k)
        multiply(k)
    act, weight = hidden()
    down_load.wait()
    lags = (0, 1, 3)
    for step in range(len(out_cuts) + lags[-1]):
        for lag, stage in zip(lags, (first, second, third)):
            if 0 <= step - lag < len(out_cuts):
                if stage is first:
                    first(0, step, act, weight)
                else:
                    stage(0, step - lag)
    for h in range(halves):
        for j in pieces:
            fourth(h, j)
    drain_gather()
    for copy in sent:
        copy.wait_send()


def fused(residual, norm_gain, expert_ids, expert_weights, gate_proj, up_proj, down_proj):
    rows, model = residual.shape
    hidden = gate_proj.shape[2]
    devices = lax.axis_size("expert")
    experts = devices // 2
    line = devices // 4
    halves = 1
    in_cuts = cuts(model, (6, 5))
    ins = len(in_cuts)
    tokens = rows * devices
    width = -(-(model + 2 * experts) // LANES) * LANES
    out_cuts = cuts(model, (2, 3, 3, 2, 1))
    outs = len(out_cuts)
    vmem = pl.BlockSpec(memory_space=pltpu.VMEM)
    hbm = pl.BlockSpec(memory_space=pl.ANY)
    dma = pltpu.SemaphoreType.DMA
    return pl.pallas_call(
        functools.partial(kernel, line, experts, in_cuts, out_cuts),
        out_shape=jax.ShapeDtypeStruct((rows, model), BF16),
        in_specs=[vmem] * 4 + [hbm] * 3,
        out_specs=vmem,
        scratch_shapes=[
            pltpu.VMEM((hidden, model), BF16),
            pltpu.VMEM((hidden, model), BF16),
            pltpu.VMEM((hidden, model), BF16),
            pltpu.VMEM((tokens, width), BF16),
            pltpu.VMEM((tokens, hidden), F32),
            pltpu.VMEM((tokens, hidden), F32),
            pltpu.VMEM((tokens, model), BF16),
            pltpu.VMEM((tokens // 2, model), BF16),
            pltpu.VMEM((tokens // 4, model), BF16),
            pltpu.VMEM((tokens // 4, model), BF16),
            pltpu.VMEM((tokens // 4, model), BF16),
            pltpu.VMEM((tokens // 4, model), BF16),
            dma((ins, 2)),
            dma,
            dma((ins, line)),
            dma((ins, line)),
            dma((ins, line)),
            dma((ins, line)),
            dma((ins, line)),
            dma((ins, 2)),
            dma((ins, 2)),
            dma((halves, outs)),
            dma((halves, outs)),
            dma((halves, outs)),
            dma((halves, outs)),
            dma((halves, outs, line)),
            dma((halves, outs, line)),
        ],
        compiler_params=pltpu.CompilerParams(
            collective_id=0, has_side_effects=True, vmem_limit_bytes=60 * 1024 * 1024
        ),
    )(
        residual, norm_gain, expert_ids.T, expert_weights.T,
        gate_proj.transpose(0, 2, 1), up_proj.transpose(0, 2, 1), down_proj,
    )


def body(residual, norm_gain, expert_ids, expert_weights, gate_proj, up_proj, down_proj):
    rows = residual.shape[0]
    devices = lax.axis_size("expert")
    capacity = 4 * rows * expert_ids.shape[1] // devices
    dense = capacity >= rows and devices % 4 == 0
    form = fused if dense else slotted
    return form(
        residual, norm_gain, expert_ids, expert_weights, gate_proj, up_proj, down_proj
    )


def solution(mesh):
    in_specs = (
        P(("groups", "expert"), None),
        P(),
        P(("groups", "expert"), None),
        P(("groups", "expert"), None),
        P("expert", None, None),
        P("expert", None, None),
        P("expert", None, None),
    )
    out_specs = P(("groups", "expert"), None)
    return jax.shard_map(body, mesh=mesh, in_specs=in_specs, out_specs=out_specs, check_vma=False)
```
